32 devices in a mesh: seq: 32 (over z, y, x, core).
Axes of the slice: x: 2, y: 2, z: 4, core: 2. Of those that a mesh axis runs over, the one named last changes fastest.
Arguments:
- parent_rows: bfloat16 [8192, 512], P('seq'), may hold values from -50 to 50, as said below
- counts: int32 [8192], P('seq'), may hold values from 0 to 8, as said below
- occupancy: int32 [16384], P('seq'), may hold values from 1 to 255
- sib_table: bfloat16 [8, 512], replicated, may hold values from -6 to 6
- gain: float32 [512], replicated, may hold values from 0.1 to 1.9
- w_qkv: bfloat16 [512, 1536], replicated, may hold values from -0.25 to 0.25
- w_out: bfloat16 [512, 512], replicated, may hold values from -0.25 to 0.25
- w_head: bfloat16 [512, 8], replicated, may hold values from -0.25 to 0.25
Outputs:
- grad_qkv: float32 [512, 1536], replicated
- grad_out: float32 [512, 512], replicated
- grad_head: float32 [512, 8], replicated
- grad_gain: float32 [512], replicated
- grad_sib: float32 [8, 512], replicated
The draws below stay inside these ranges and needn't reach their ends.
Inputs may be any that keep to these rules, and one draw needn't show every extreme that they name: `parent_rows`: each value is a random draw times a scale of its row and a scale of its column. The counts add up to 16384. The children of the parents held by device k form the contiguous range of nodes given by the counts, and lie on devices k-1, k and k+1. In each device's 256 parents, some parent has 8 children and some has none.
All inputs are finite; a program needn't handle non-finite values.
Results may differ from the reference program's by a relative error of at most 0.0045.
Values may be sent and summed in bfloat16 or wider, within the bound.
No kernel may reach another device: no remote copies, remote signals or barrier semaphores. Data moves between devices by JAX's collectives and lax.ppermute only.
A program may use at most 128 MiB of HBM per device.

```python
import math
import jax
import jax.numpy as jnp
from jax import lax

D = 512
HEADS = 4
BITS = 8
OCTANTS = 8
NODE_DEV = 512
PAR_DEV = 256
NODES = 16384
PARENTS = 8192


def draw_parent_rows(key, part):
    own_key = jax.random.fold_in(key, 11)
    first, second, third = jax.random.split(own_key, 3)
    base = jnp.clip(jax.random.normal(first, (PARENTS, D), jnp.float32), -5.0, 5.0)
    row_scale = jnp.exp(jax.random.uniform(second, (PARENTS, 1), jnp.float32, 0.0, math.log(10.0)))
    col_scale = jnp.exp(jax.random.uniform(third, (1, D), jnp.float32, 0.0, math.log(10.0)))
    return (base * row_scale * col_scale * 0.1).astype(jnp.bfloat16)


def draw_counts(key, part):
    own_key = jax.random.fold_in(key, 23)
    blocks = PARENTS // PAR_DEV
    quarter = NODE_DEV // 4
    first, second, third = jax.random.split(own_key, 3)
    excess = jax.random.randint(first, (blocks,), -quarter, quarter + 1).astype(jnp.int32)
    places = jnp.arange(blocks)
    excess = jnp.where(places == 0, quarter, jnp.where(places == 1, -quarter, excess))
    excess = jnp.where(places == blocks - 1, 0, excess).astype(jnp.int32)
    before = jnp.concatenate([jnp.zeros((1,), jnp.int32), excess[:-1]])
    totals = NODE_DEV + excess - before
    full_bins = jax.random.randint(second, (blocks,), 0, PAR_DEV).astype(jnp.int32)
    block_keys = jax.random.split(third, blocks)
    slots = 8 * PAR_DEV

    def one_block(block_key, total, full_bin):
        ranks = jax.random.permutation(block_key, slots).astype(jnp.int32)
        bin_of = jnp.arange(slots, dtype=jnp.int32) // 8
        empty_bin = (full_bin + 1) % PAR_DEV
        special = (bin_of == full_bin) | (bin_of == empty_bin)
        taken = jnp.concatenate([jax.lax.dynamic_slice_in_dim(ranks, full_bin * 8, 8), jax.lax.dynamic_slice_in_dim(ranks, empty_bin * 8, 8)])
        below = jnp.sum((taken[None, :] < ranks[:, None]).astype(jnp.int32), axis=1)
        other_rank = ranks - below
        chosen = (bin_of == full_bin) | jnp.logical_not(special) & (other_rank < total - 8)
        return jnp.sum(chosen.reshape(PAR_DEV, 8).astype(jnp.int32), axis=1)
    return jax.vmap(one_block)(block_keys, totals, full_bins).reshape(PARENTS).astype(jnp.int32)


def set_ends(entries, stream_key, low, high):
    place = [jax.random.randint(jax.random.fold_in(stream_key, axis), (), 0, length) for axis, length in enumerate(entries.shape)]
    longest = entries.shape.index(max(entries.shape))
    next_to = place[:longest] + [(place[longest] + 1) % entries.shape[longest]] + place[longest + 1:]
    return entries.at[tuple(place)].set(low).at[tuple(next_to)].set(high)


def bell_draw(key, shape, deviation, reach, held_as=jnp.bfloat16):
    return jnp.clip(deviation * jax.random.normal(key, shape, jnp.float32), -reach, reach).astype(held_as)


def setup_inputs(seed: int = 0) -> dict:
    seeds = jax.random.split(jax.random.key(seed), 9)
    return {
        "parent_rows": draw_parent_rows(jax.random.fold_in(seeds[8], 71), 0),
        "counts": draw_counts(jax.random.fold_in(seeds[8], 71), 0),
        "occupancy": set_ends(jax.random.randint(seeds[2], (NODES,), 1, 256), jax.random.fold_in(seeds[2], 1), 1, 255).astype(jnp.int32),
        "sib_table": bell_draw(seeds[3], (OCTANTS, D), 1.0, 6.0),
        "gain": jnp.clip(1.0 + 0.18 * jax.random.normal(seeds[4], (D,), jnp.float32), 0.1, 1.9),
        "w_qkv": bell_draw(seeds[5], (D, 3 * D), D ** -0.5, 0.25),
        "w_out": bell_draw(seeds[6], (D, D), D ** -0.5, 0.25),
        "w_head": bell_draw(seeds[7], (D, BITS), D ** -0.5, 0.25),
    }


highest = lax.Precision.HIGHEST

def head_slice(packed, part, head_id, width):
    head_size = width // HEADS
    begin = part * width + head_id * head_size
    return packed[:, begin:begin + head_size]

def normalize_inputs(inputs, gain):
    inputs_f = inputs.astype(jnp.float32)
    inv_in = lax.rsqrt(lax.optimization_barrier(jnp.mean(inputs_f * inputs_f, axis=-1, keepdims=True)) + 1e-06)
    normed = (inputs_f * inv_in * gain).astype(jnp.bfloat16)
    return (inputs_f, inv_in, normed)

def local_states(packed, width):
    return jnp.stack([jnp.dot(head_slice(packed, 1, head_id, width).T, head_slice(packed, 2, head_id, width), preferred_element_type=jnp.float32) for head_id in range(HEADS)])

def query_states(packed, grads, width):
    return jnp.stack([jnp.dot(head_slice(packed, 0, head_id, width).T, grads[head_id], preferred_element_type=jnp.float32) for head_id in range(HEADS)])

def causal_mask(count):
    return jnp.tril(jnp.ones((count, count), jnp.bool_))

def attend(packed, prefix, width):
    causal = causal_mask(packed.shape[0])
    scores = []
    numers = []
    inverses = []
    pieces = []
    for head_id in range(HEADS):
        queries = head_slice(packed, 0, head_id, width)
        keys_here = head_slice(packed, 1, head_id, width)
        values_here = head_slice(packed, 2, head_id, width)
        score = jnp.where(causal, jnp.dot(queries, keys_here.T, preferred_element_type=jnp.float32), 0.0)
        numer = jnp.dot(score, values_here.astype(jnp.float32), precision=highest) + jnp.dot(queries.astype(jnp.float32), prefix[head_id], precision=highest)
        inverse = lax.rsqrt(lax.optimization_barrier(jnp.mean(numer * numer, axis=-1, keepdims=True)) + 1e-05)
        scores.append(score)
        numers.append(numer)
        inverses.append(inverse)
        pieces.append(numer * inverse)
    attended = jnp.concatenate(pieces, axis=1).astype(jnp.bfloat16)
    return (scores, numers, inverses, attended)

def readout(inputs_f, attended, w_out, w_head):
    resid = inputs_f + jnp.dot(attended, w_out, preferred_element_type=jnp.float32)
    inv_out = lax.rsqrt(lax.optimization_barrier(jnp.mean(resid * resid, axis=-1, keepdims=True)) + 1e-06)
    final = (resid * inv_out).astype(jnp.bfloat16)
    logits = jnp.dot(final, w_head, preferred_element_type=jnp.float32)
    return (resid, inv_out, final, logits)

def output_grads(occupancy, logits, final, resid, inv_out, w_head, scale):
    powers = 2 ** jnp.arange(w_head.shape[1], dtype=jnp.int32)
    target = (occupancy[:, None] // powers[None, :] % 2).astype(jnp.float32)
    d_logits = ((jax.nn.sigmoid(logits) - target) * scale).astype(jnp.bfloat16)
    grad_head = jnp.dot(final.T, d_logits, preferred_element_type=jnp.float32)
    d_final = jnp.dot(d_logits, w_head.T, preferred_element_type=jnp.float32)
    d_resid = inv_out * d_final - resid * inv_out ** 3 * lax.optimization_barrier(jnp.mean(d_final * resid, axis=-1, keepdims=True))
    return (grad_head, d_resid)

def numer_grads(attended, d_resid, numers, inverses, w_out, width):
    d_resid_b = d_resid.astype(jnp.bfloat16)
    grad_out = jnp.dot(attended.T, d_resid_b, preferred_element_type=jnp.float32)
    d_attended = jnp.dot(d_resid_b, w_out.T, preferred_element_type=jnp.float32)
    head_size = width // HEADS
    grads = []
    for head_id in range(HEADS):
        piece = d_attended[:, head_id * head_size:(head_id + 1) * head_size]
        numer = numers[head_id]
        inverse = inverses[head_id]
        d_numer = inverse * piece - numer * inverse ** 3 * lax.optimization_barrier(jnp.mean(piece * numer, axis=-1, keepdims=True))
        grads.append(d_numer.astype(jnp.bfloat16))
    return (grad_out, grads)

def attention_grads(packed, scores, grads, prefix, suffix, width):
    causal = causal_mask(packed.shape[0])
    d_queries = []
    d_keys = []
    d_values = []
    for head_id in range(HEADS):
        queries = head_slice(packed, 0, head_id, width)
        keys_here = head_slice(packed, 1, head_id, width)
        values_here = head_slice(packed, 2, head_id, width)
        grad = grads[head_id]
        grad_f = grad.astype(jnp.float32)
        back = jnp.where(causal, jnp.dot(grad, values_here.T, preferred_element_type=jnp.float32), 0.0)
        d_queries.append(jnp.dot(back, keys_here.astype(jnp.float32), precision=highest) + jnp.dot(grad_f, prefix[head_id].T, precision=highest))
        d_keys.append(jnp.dot(back.T, queries.astype(jnp.float32), precision=highest) + jnp.dot(values_here.astype(jnp.float32), suffix[head_id].T, precision=highest))
        d_values.append(jnp.dot(scores[head_id].T, grad_f, precision=highest) + jnp.dot(keys_here.astype(jnp.float32), suffix[head_id], precision=highest))
    return jnp.concatenate(d_queries + d_keys + d_values, axis=1).astype(jnp.bfloat16)

def input_grads(inputs_f, inv_in, normed, d_packed, d_resid, onehot, gain, w_qkv):
    grad_qkv = jnp.dot(normed.T, d_packed, preferred_element_type=jnp.float32)
    d_normed = jnp.dot(d_packed, w_qkv.T, preferred_element_type=jnp.float32)
    grad_gain = lax.optimization_barrier(jnp.sum(d_normed * inputs_f * inv_in, axis=0))
    d_scaled = d_normed * gain
    d_inputs = inv_in * d_scaled - inputs_f * inv_in ** 3 * lax.optimization_barrier(jnp.mean(d_scaled * inputs_f, axis=-1, keepdims=True)) + d_resid
    grad_sib = jnp.dot(onehot.T, d_inputs, precision=highest)
    return (grad_qkv, grad_gain, grad_sib)

def reference(parent_rows, counts, occupancy, sib_table, gain, w_qkv, w_out, w_head):
    width = parent_rows.shape[1]
    ends = jnp.cumsum(counts).astype(jnp.int32)
    starts = ends - counts
    node_ids = jnp.arange(NODES, dtype=jnp.int32)
    parent_of = jnp.searchsorted(ends, node_ids, side='right').astype(jnp.int32)
    rank = node_ids - starts[parent_of]
    onehot = (rank[:, None] == jnp.arange(sib_table.shape[0], dtype=jnp.int32)[None, :]).astype(jnp.float32)
    inputs = (parent_rows[parent_of].astype(jnp.float32) + jnp.dot(onehot.astype(jnp.bfloat16), sib_table, preferred_element_type=jnp.float32)).astype(jnp.bfloat16)
    blocks = NODES // NODE_DEV
    inputs_b = inputs.reshape(blocks, NODE_DEV, width)
    onehot_b = onehot.reshape(blocks, NODE_DEV, onehot.shape[1])
    occupancy_b = occupancy.reshape(blocks, NODE_DEV)
    scale = float(NODES) ** (-0.5)

    def first_pass(block):
        inputs_f, inv_in, normed = normalize_inputs(block, gain)
        packed = jnp.dot(normed, w_qkv, preferred_element_type=jnp.float32).astype(jnp.bfloat16)
        return (packed, local_states(packed, width))
    packed_b, states_b = lax.map(first_pass, inputs_b)
    prefix_b = jnp.concatenate([jnp.zeros_like(states_b[:1]), jnp.cumsum(states_b, axis=0)[:-1]], axis=0)

    def second_pass(items):
        block, packed, prefix, occ = items
        inputs_f, inv_in, normed = normalize_inputs(block, gain)
        scores, numers, inverses, attended = attend(packed, prefix, width)
        resid, inv_out, final, logits = readout(inputs_f, attended, w_out, w_head)
        grad_head, d_resid = output_grads(occ, logits, final, resid, inv_out, w_head, scale)
        grad_out, grads = numer_grads(attended, d_resid, numers, inverses, w_out, width)
        return (grad_head, grad_out, d_resid, jnp.stack(grads), query_states(packed, grads, width))
    head_b, out_b, resid_grad_b, grads_b, qstates_b = lax.map(second_pass, (inputs_b, packed_b, prefix_b, occupancy_b))
    suffix_b = jnp.concatenate([jnp.cumsum(qstates_b[::-1], axis=0)[::-1][1:], jnp.zeros_like(qstates_b[:1])], axis=0)

    def third_pass(carry, items):
        block, packed, prefix, suffix, grads, d_resid, onehot_here = items
        inputs_f, inv_in, normed = normalize_inputs(block, gain)
        scores, numers, inverses, attended = attend(packed, prefix, width)
        d_packed = attention_grads(packed, scores, grads, prefix, suffix, width)
        parts = input_grads(inputs_f, inv_in, normed, d_packed, d_resid, onehot_here, gain, w_qkv)
        return ((carry[0] + parts[0], carry[1] + parts[1], carry[2] + parts[2]), None)
    start = (jnp.zeros((width, 3 * width), jnp.float32), jnp.zeros((width,), jnp.float32), jnp.zeros((sib_table.shape[0], width), jnp.float32))
    totals, unused = lax.scan(third_pass, start, (inputs_b, packed_b, prefix_b, suffix_b, grads_b, resid_grad_b, onehot_b))
    return (totals[0], lax.optimization_barrier(jnp.sum(out_b, axis=0)), lax.optimization_barrier(jnp.sum(head_b, axis=0)), totals[1], totals[2])
```

```python
import functools

import jax
import jax.numpy as jnp
from jax import lax
from jax.experimental import pallas as pl
from jax.experimental.pallas import tpu as pltpu
from jax.sharding import PartitionSpec as P

HEADS = 4
F32 = jnp.float32
BF16 = jnp.bfloat16


def stages_of(count):
    found, stride = [], 1
    while stride < count:
        left = count // stride
        radix = 2 if stride == 1 and left % 2 == 0 else 4 if left % 4 == 0 else 2 if left % 2 == 0 else left
        found.append((stride, radix))
        stride *= radix
    return found


def partners(count, stride, radix):
    pairs = []
    for b in range(1, radix):
        pairs.append([(i, i ^ (b * stride)) for i in range(count)])
    return pairs


def swap(value, stride, radix):
    count = lax.axis_size("seq")
    return [lax.ppermute(value, "seq", pairs) for pairs in partners(count, stride, radix)]


def swap_each(values, stride, radix):
    count = lax.axis_size("seq")
    return [
        lax.ppermute(value, "seq", pairs)
        for value, pairs in zip(values, partners(count, stride, radix))
    ]


def digit(stride, radix):
    return lax.axis_index("seq") // stride % radix


def pair_sum(values):
    while len(values) > 1:
        values = [
            values[i] + values[i + 1] if i + 1 < len(values) else values[i]
            for i in range(0, len(values), 2)
        ]
    return values[0]


def offset_of(total):
    before = jnp.zeros_like(total)
    for stride, radix in stages_of(lax.axis_size("seq")):
        heard = swap(total, stride, radix)
        mine = digit(stride, radix)
        for b, value in enumerate(heard, 1):
            before = before + jnp.where(mine ^ b < mine, value, 0)
        total = total + sum(heard)
    return before


def scan_states(states, later):
    stages = stages_of(lax.axis_size("seq"))
    rows = states.shape[0] // 2
    core = digit(*stages[0])
    other = swap(states, *stages[0])[0]
    own = lax.dynamic_slice_in_dim(states, core * rows, rows, 0).astype(F32)
    total = own + lax.dynamic_slice_in_dim(other, core * rows, rows, 0).astype(F32)
    before = jnp.zeros_like(total)
    for place, (stride, radix) in enumerate(stages[1:]):
        heard = swap(total.astype(BF16), stride, radix)
        mine = digit(stride, radix)
        for b, value in enumerate(heard, 1):
            theirs = mine ^ b
            counts = theirs > mine if later else theirs < mine
            before = before + jnp.where(counts, value.astype(F32), 0.0)
        total = total + sum(value.astype(F32) for value in heard)
    half = before.astype(BF16)
    far = swap(half, *stages[0])[0]
    first = jnp.where(core == 0, half, far).astype(F32)
    second = jnp.where(core == 0, far, half).astype(F32)
    whole = jnp.concatenate([first, second], axis=0)
    near = core == 0 if later else core == 1
    return (whole + jnp.where(near, other.astype(F32), 0.0)).astype(BF16)


def small_sum(value):
    for stride, radix in stages_of(lax.axis_size("seq")):
        value = pair_sum([value] + swap(value, stride, radix))
    return value


def dot(a, b):
    return lax.dot_general(a, b, (((1,), (0,)), ((), ())), preferred_element_type=F32)


def dot_nt(a, b):
    return lax.dot_general(a, b, (((1,), (1,)), ((), ())), preferred_element_type=F32)


def dot_tn(a, b):
    return lax.dot_general(a, b, (((0,), (0,)), ((), ())), preferred_element_type=F32)


def call(kernel, outs, *args, smem=(), name=None):
    in_specs = [
        pl.BlockSpec(memory_space=pltpu.SMEM if i in smem else pltpu.VMEM)
        for i in range(len(args))
    ]
    return pl.pallas_call(
        kernel,
        out_shape=[jax.ShapeDtypeStruct(shape, dtype) for shape, dtype in outs],
        in_specs=in_specs,
        out_specs=[pl.BlockSpec(memory_space=pltpu.VMEM) for _ in outs],
        compiler_params=pltpu.CompilerParams(vmem_limit_bytes=48 * 1024 * 1024),
        name=name,
    )(*args)


def tril(count):
    row = lax.broadcasted_iota(jnp.int32, (count, count), 0)
    col = lax.broadcasted_iota(jnp.int32, (count, count), 1)
    return row >= col


def embed_kernel(
    shift, low, mid, high, bounds, sib, gain, w_qkv, inputs_o, normed_o, rank_o, packed_o, states_o
):
    nodes = inputs_o.shape[0]
    width = inputs_o.shape[1]
    head = width // HEADS
    parents = mid.shape[0]
    starts = bounds[0:1, :] + shift[0]
    ends = bounds[1:2, :] + shift[0]
    node = lax.broadcasted_iota(jnp.int32, (nodes, starts.shape[1]), 0)
    begun = starts <= node
    held = jnp.where(begun & (node < ends), 1.0, 0.0).astype(BF16)
    start = jnp.max(jnp.where(begun, starts, -(2**30)), axis=1, keepdims=True)
    lanes = lax.broadcasted_iota(jnp.int32, (nodes, 128), 1)
    rank = lax.broadcasted_iota(jnp.int32, (nodes, 128), 0) - start
    onehot = jnp.where(rank == lanes, 1.0, 0.0).astype(BF16)
    rank_o[...] = onehot
    feat = dot(held[:, :parents], low[...])
    feat = feat + dot(held[:, parents : 2 * parents], mid[...])
    feat = feat + dot(held[:, 2 * parents :], high[...])
    feat = feat + dot(onehot[:, : sib.shape[0]], sib[...])
    inputs = feat.astype(BF16)
    inputs_o[...] = inputs
    x = inputs.astype(F32)
    inv = lax.rsqrt(jnp.mean(x * x, axis=-1, keepdims=True) + 1e-06)
    normed = (x * inv * gain[...]).astype(BF16)
    normed_o[...] = normed
    packed = dot(normed, w_qkv[...]).astype(BF16)
    packed_o[...] = packed
    for h in range(HEADS):
        k = packed[:, width + h * head : width + (h + 1) * head]
        v = packed[:, 2 * width + h * head : 2 * width + (h + 1) * head]
        states_o[h * head : (h + 1) * head, :] = dot_tn(k, v).astype(BF16)


def local_kernel(packed, numer_o):
    nodes, width = numer_o.shape
    head = width // HEADS
    causal = tril(nodes)
    for h in range(HEADS):
        q = packed[:, h * head : (h + 1) * head]
        k = packed[:, width + h * head : width + (h + 1) * head]
        v = packed[:, 2 * width + h * head : 2 * width + (h + 1) * head]
        score = jnp.where(causal, dot_nt(q, k), 0.0).astype(BF16)
        numer_o[:, h * head : (h + 1) * head] = dot(score, v)


def loss_kernel(
    scale, packed, local, prefix, inputs, occupancy, w_out, w_head,
    attended_o, d_resid_o, grads_o, states_o, head_o,
):
    nodes, width = local.shape
    head = width // HEADS
    nhats, invs = [], []
    for h in range(HEADS):
        cols = slice(h * head, (h + 1) * head)
        numer = local[:, cols] + dot(packed[:, cols], prefix[cols, :])
        inv = lax.rsqrt(jnp.mean(numer * numer, axis=-1, keepdims=True) + 1e-05)
        nhat = numer * inv
        nhats.append(nhat)
        invs.append(inv)
        attended_o[:, cols] = nhat.astype(BF16)
    resid = inputs[...].astype(F32) + dot(attended_o[...], w_out[...])
    inv_out = lax.rsqrt(jnp.mean(resid * resid, axis=-1, keepdims=True) + 1e-06)
    normal = resid * inv_out
    final = normal.astype(BF16)
    logits = dot(final, w_head[...])
    bits = lax.broadcasted_iota(jnp.int32, logits.shape, 1)
    target = (jnp.right_shift(occupancy[...], bits) & 1).astype(F32)
    d_logits = ((jax.nn.sigmoid(logits) - target) * scale).astype(BF16)
    head_o[...] = dot_tn(d_logits, final)
    d_final = dot_nt(d_logits, w_head[...])
    d_resid = inv_out * (d_final - normal * jnp.mean(d_final * normal, axis=-1, keepdims=True))
    d_resid_o[...] = d_resid
    d_att = dot_nt(d_resid.astype(BF16), w_out[...])
    for h in range(HEADS):
        cols = slice(h * head, (h + 1) * head)
        e = d_att[:, cols]
        g = invs[h] * (e - nhats[h] * jnp.mean(e * nhats[h], axis=-1, keepdims=True))
        g = g.astype(BF16)
        grads_o[:, cols] = g
        states_o[cols, :] = dot_tn(packed[:, cols], g).astype(BF16)


def back_kernel(
    core, packed, grads, prefix, normed, attended, d_resid, w_q,
    dk_o, dv_o, d_normed_o, keep_o, send_o, whole,
):
    nodes, width = grads.shape
    head = width // HEADS
    causal = tril(nodes)
    dqs = []
    for h in range(HEADS):
        cols = slice(h * head, (h + 1) * head)
        q = packed[:, cols]
        k = packed[:, width + h * head : width + (h + 1) * head]
        v = packed[:, 2 * width + h * head : 2 * width + (h + 1) * head]
        g = grads[:, cols]
        back = jnp.where(causal, dot_nt(g, v), 0.0).astype(BF16)
        dqs.append((dot(back, k) + dot_nt(g, prefix[cols, :])).astype(BF16))
        dk_o[:, cols] = dot_tn(back, q)
        score = jnp.where(causal, dot_nt(q, k), 0.0).astype(BF16)
        dv_o[:, cols] = dot_tn(score, g)
    dq = jnp.concatenate(dqs, axis=1)
    d_normed_o[...] = dot_nt(dq, w_q[...])
    whole[:, :width] = dot_tn(normed[...], dq)
    whole[:, width:] = dot_tn(attended[...], d_resid[...].astype(BF16))
    split(core[0], whole, keep_o, send_o)


def split(core, whole, keep_o, send_o):
    rows = keep_o.shape[0]
    keep_o[...] = whole[pl.ds(pl.multiple_of(core * rows, rows), rows), :]
    send_o[...] = whole[pl.ds(pl.multiple_of((1 - core) * rows, rows), rows), :]


def last_kernel(
    core, packed, dk, dv, suffix, normed, inputs, d_normed_q, d_resid, rank, gain, w_kv,
    keep_o, send_o, gain_o, sib_o, whole,
):
    nodes, width = dk.shape
    head = width // HEADS
    dks, dvs = [], []
    for h in range(HEADS):
        cols = slice(h * head, (h + 1) * head)
        k = packed[:, width + h * head : width + (h + 1) * head]
        v = packed[:, 2 * width + h * head : 2 * width + (h + 1) * head]
        dks.append((dk[:, cols] + dot_nt(v, suffix[cols, :])).astype(BF16))
        dvs.append((dv[:, cols] + dot(k, suffix[cols, :])).astype(BF16))
    both = jnp.concatenate(dks + dvs, axis=1)
    whole[...] = dot_tn(normed[...], both)
    split(core[0], whole, keep_o, send_o)
    d_normed = d_normed_q[...] + dot_nt(both, w_kv[...])
    x = inputs[...].astype(F32)
    inv = lax.rsqrt(jnp.mean(x * x, axis=-1, keepdims=True) + 1e-06)
    unit = x * inv
    gain_o[...] = jnp.sum(d_normed * unit, axis=0, keepdims=True)
    s = d_normed * gain[...]
    d_inputs = inv * (s - unit * jnp.mean(s * unit, axis=-1, keepdims=True)) + d_resid[...]
    upper = d_inputs.astype(BF16)
    lower = (d_inputs - upper.astype(F32)).astype(BF16)
    onehot = rank[...]
    sib_o[...] = (dot_tn(onehot, upper) + dot_tn(onehot, lower))[: sib_o.shape[0], :]


def chunks_kernel(radix, place, *refs):
    held, heard, own, outs = refs[0], refs[1 : -radix], refs[-radix], refs[-radix + 1 :]
    rows = own.shape[0]
    for b in range(radix):
        at = pl.ds(pl.multiple_of((place[0] ^ b) * rows, rows), rows)
        value = pair_sum([held[at, :]] + [piece[at, :].astype(F32) for piece in heard])
        if b == 0:
            own[...] = value
        else:
            outs[b - 1][...] = value.astype(BF16)


def scatter_step(held, heard, stride, radix):
    rows, cols = held.shape[0] // radix, held.shape[1]
    outs = [((rows, cols), F32)] + [((rows, cols), BF16)] * (radix - 1)
    place = digit(stride, radix).astype(jnp.int32).reshape(1)
    got = call(
        functools.partial(chunks_kernel, radix), outs, place, held, *heard, smem=(0,), name="chunks"
    )
    return got[0], swap_each(got[1:], stride, radix)


def reduce_scatter(keep, send):
    stages = stages_of(lax.axis_size("seq"))
    held, heard = keep, swap(send, *stages[0])
    used = []
    for stride, radix in stages[1:]:
        if held.shape[0] % (16 * radix) == 0:
            held, heard = scatter_step(held, heard, stride, radix)
            used.append((stride, radix))
        else:
            held = pair_sum([held] + [piece.astype(F32) for piece in heard])
            heard = swap(held, stride, radix)
    piece = pair_sum([held] + [value.astype(F32) for value in heard]).astype(BF16)
    return piece, used


def gather(piece, used):
    for stride, radix in reversed(used):
        piece = jnp.concatenate([piece] + swap(piece, stride, radix), axis=0)
    return piece, swap(piece, *stages_of(lax.axis_size("seq"))[0])[0]


def place_kernel(radices, core, digits, first, first_far, second, second_far, qkv_o, out_o):
    width = out_o.shape[1]
    half = first.shape[0]
    blocks = 1
    for radix in radices:
        blocks *= radix
    rows = half // blocks
    for index in range(blocks):
        left, target, size = index, 0, half
        spans = []
        inner = blocks
        for stage, radix in enumerate(radices):
            inner //= radix
            b = left // inner
            left = left % inner
            size = size // radix
            target = target + (digits[stage] ^ b) * size
        src = slice(index * rows, (index + 1) * rows)
        near = pl.ds(pl.multiple_of(core[0] * half + target, rows), rows)
        far = pl.ds(pl.multiple_of((1 - core[0]) * half + target, rows), rows)
        for at, one, two in ((near, first, second), (far, first_far, second_far)):
            qkv_o[at, :width] = one[src, :width].astype(F32)
            out_o[at, :] = one[src, width:].astype(F32)
            qkv_o[at, width:] = two[src, :].astype(F32)


def shards(parent_rows, counts, occupancy, sib_table, gain, w_qkv, w_out, w_head):
    count = lax.axis_size("seq")
    index = lax.axis_index("seq")
    parents = counts.shape[0]
    nodes = occupancy.shape[0]
    width = parent_rows.shape[1]
    bits = w_head.shape[1]
    octants = sib_table.shape[0]
    up = [(i, i + 1) for i in range(count - 1)]
    down = [(i + 1, i) for i in range(count - 1)]
    core = (index % 2).astype(jnp.int32).reshape(1)

    row = counts.reshape(1, parents)
    row_low = lax.ppermute(row, "seq", up)
    row_high = lax.ppermute(row, "seq", down)
    rows_low = lax.ppermute(parent_rows, "seq", up)
    rows_high = lax.ppermute(parent_rows, "seq", down)
    total = jnp.broadcast_to(jnp.sum(counts), (1, 128))
    offset = offset_of(total)[0, 0]

    window = jnp.concatenate([row_low, row, row_high], axis=1)
    ends = jnp.cumsum(window, axis=1) - jnp.sum(row_low)
    bounds = jnp.concatenate([ends - window, ends], axis=0)
    shift = (offset - index * nodes).astype(jnp.int32).reshape(1)
    gain_row = gain.reshape(1, width)

    inputs, normed, rank, packed, states = call(
        embed_kernel,
        [
            ((nodes, width), BF16),
            ((nodes, width), BF16),
            ((nodes, 128), BF16),
            ((nodes, 3 * width), BF16),
            ((width, width // HEADS), BF16),
        ],
        shift, rows_low, parent_rows, rows_high, bounds, sib_table, gain_row, w_qkv,
        smem=(0,),
        name="embed",
    )
    (local,) = call(local_kernel, [((nodes, width), F32)], packed, name="local")
    prefix = scan_states(states, False)

    scale = float(count * nodes) ** (-0.5)
    attended, d_resid, grads, qstates, grad_head = call(
        functools.partial(loss_kernel, scale),
        [
            ((nodes, width), BF16),
            ((nodes, width), F32),
            ((nodes, width), BF16),
            ((width, width // HEADS), BF16),
            ((bits, width), F32),
        ],
        packed, local, prefix, inputs, occupancy.reshape(nodes, 1), w_out, w_head,
        name="loss",
    )
    suffix = scan_states(qstates, True)

    def call_split(kernel, outs, *args, name):
        in_specs = [pl.BlockSpec(memory_space=pltpu.SMEM)] + [
            pl.BlockSpec(memory_space=pltpu.VMEM) for _ in args[1:]
        ]
        return pl.pallas_call(
            kernel,
            out_shape=[jax.ShapeDtypeStruct(shape, dtype) for shape, dtype in outs],
            in_specs=in_specs,
            out_specs=[pl.BlockSpec(memory_space=pltpu.VMEM) for _ in outs],
            scratch_shapes=[pltpu.VMEM((width, 2 * width), F32)],
            compiler_params=pltpu.CompilerParams(vmem_limit_bytes=48 * 1024 * 1024),
            name=name,
        )(*args)

    halves = [((width // 2, 2 * width), F32)] * 2
    dk, dv, d_normed_q, keep_1, send_1 = call_split(
        back_kernel,
        [((nodes, width), F32)] * 3 + halves,
        core, packed, grads, prefix, normed, attended, d_resid, w_qkv[:, :width],
        name="back",
    )
    piece_1, used = reduce_scatter(keep_1, send_1)
    first, first_far = gather(piece_1, used)

    keep_2, send_2, grad_gain, grad_sib = call_split(
        last_kernel,
        halves + [((1, width), F32), ((octants, width), F32)],
        core, packed, dk, dv, suffix, normed, inputs, d_normed_q, d_resid, rank, gain_row, w_qkv[:, width:],
        name="last",
    )
    piece_2, used = reduce_scatter(keep_2, send_2)
    second, second_far = gather(piece_2, used)
    small = small_sum(jnp.concatenate([grad_head, grad_sib, grad_gain], axis=0))

    digits = jnp.stack([digit(stride, radix) for stride, radix in used]).astype(jnp.int32)
    grad_qkv, grad_out = call(
        functools.partial(place_kernel, [radix for _, radix in used]),
        [((width, 3 * width), F32), ((width, width), F32)],
        core, digits, first, first_far, second, second_far,
        smem=(0, 1),
        name="place",
    )
    return (
        grad_qkv,
        grad_out,
        small[:bits].T,
        small[bits + octants],
        small[bits : bits + octants],
    )


def solution(mesh):
    placed = (P("seq", None), P("seq"), P("seq"), P(), P(), P(), P(), P())
    return jax.shard_map(
        shards, mesh=mesh, in_specs=placed, out_specs=(P(), P(), P(), P(), P()), check_vma=False
    )
```

```python
import functools

import jax
import jax.numpy as jnp
from jax import lax
from jax.experimental import pallas as pl
from jax.experimental.pallas import tpu as pltpu
from jax.sharding import PartitionSpec as P

HEADS = 4
BITS = 8
GAIN_AT = 8
HEAD_AT = 16
F32 = jnp.float32
BF16 = jnp.bfloat16


def stages_of(count):
    found, stride = [], 1
    while stride < count:
        left = count // stride
        radix = 2 if stride == 1 and left % 2 == 0 else 4 if left % 4 == 0 else 2 if left % 2 == 0 else left
        found.append((stride, radix))
        stride *= radix
    return found


def partners(count, stride, radix):
    pairs = []
    for b in range(1, radix):
        pairs.append([(i, i ^ (b * stride)) for i in range(count)])
    return pairs


def swap(value, stride, radix):
    count = lax.axis_size("seq")
    return [lax.ppermute(value, "seq", pairs) for pairs in partners(count, stride, radix)]


def swap_each(values, stride, radix):
    count = lax.axis_size("seq")
    return [
        lax.ppermute(value, "seq", pairs)
        for value, pairs in zip(values, partners(count, stride, radix))
    ]


def digit(stride, radix):
    return lax.axis_index("seq") // stride % radix


def pair_sum(values):
    while len(values) > 1:
        values = [
            values[i] + values[i + 1] if i + 1 < len(values) else values[i]
            for i in range(0, len(values), 2)
        ]
    return values[0]


def count_of(tile):
    return tile[:8].astype(F32) * 256.0 + tile[8:16].astype(F32)


def digits_of(number):
    upper = jnp.floor(number * (1.0 / 256.0))
    return jnp.concatenate([upper, number - 256.0 * upper], axis=0).astype(BF16)


def post(total, message):
    rows = total.shape[0] // 128 * 128
    message[:rows, :] = total[:rows, :].astype(BF16)
    if rows < total.shape[0]:
        message[rows:, :] = digits_of(total[rows:, :])


def chip_kernel(states, other, total, message):
    rows = states.shape[0] // 256 * 128
    at = pl.ds(pl.multiple_of(digit(1, 2) * rows, rows), rows)
    total[:rows, :] = states[at, :].astype(F32) + other[at, :].astype(F32)
    if rows < total.shape[0]:
        total[rows:, :] = count_of(states[2 * rows :, :]) + count_of(other[2 * rows :, :])
    post(total, message)


def stage_kernel(stride, radix, later, first, last, *refs):
    refs = list(refs)
    total, heard = refs[0], refs[1:radix]
    refs = refs[radix:]
    before = None if first else refs.pop(0)
    sums, message = refs[0], refs[-1]
    mine = digit(stride, radix)
    rows = total.shape[0] // 128 * 128
    for at, read in ((slice(0, rows), lambda v: v[:rows, :].astype(F32)), (slice(rows, None), lambda v: count_of(v[rows:, :]))):
        if at.start == total.shape[0]:
            continue
        part = None if first else before[at, :]
        whole = total[at, :]
        for b, value in enumerate(heard, 1):
            theirs = mine ^ b
            counts = theirs > mine if later else theirs < mine
            value = read(value)
            whole = whole + value
            value = jnp.where(counts, value, 0.0)
            part = value if part is None else part + value
        sums[at, :] = part
        if not last:
            refs[1][at, :] = whole
    if last:
        message[...] = sums[:rows, :].astype(BF16)
    else:
        post(refs[1], message)


def scan_states(states, later, counted):
    stages = stages_of(lax.axis_size("seq"))
    rows = states.shape[0] // 256 * 128
    other = swap(states, *stages[0])[0]
    kept = ((rows + (8 if counted else 0), 128), F32)
    sent = ((rows + (16 if counted else 0), 128), BF16)
    total, message = call(chip_kernel, [kept, sent], states, other, name="chip", mib=4)
    before = []
    for place, (stride, radix) in enumerate(stages[1:], 2):
        last = place == len(stages)
        heard = swap(message, stride, radix)
        got = call(
            functools.partial(stage_kernel, stride, radix, later, not before, last),
            [kept, ((rows, 128), BF16)] if last else [kept, kept, sent],
            total, *heard, *before,
            name="stage",
            mib=4,
        )
        before, message = [got[0]], got[-1]
        total = got[1]
    return before[0], swap(message, *stages[0])[0], other


def dot(a, b):
    return lax.dot_general(a, b, (((1,), (0,)), ((), ())), preferred_element_type=F32)


def dot_nt(a, b):
    return lax.dot_general(a, b, (((1,), (1,)), ((), ())), preferred_element_type=F32)


def dot_tn(a, b):
    return lax.dot_general(a, b, (((0,), (0,)), ((), ())), preferred_element_type=F32)


class Arriving:
    def __init__(self, source, target, sem):
        self.target, self.shape = target, target.shape
        self.copy = pltpu.make_async_copy(source, target, sem)
        self.copy.start()

    def ready(self):
        if self.copy is not None:
            self.copy.wait()
            self.copy = None
        return self.target

    def __getitem__(self, at):
        return self.ready()[at]


def call(kernel, outs, *args, hbm=(), scratch=(), name=None, mib=16):
    args = [
        pltpu.with_memory_space_constraint(value, pltpu.HBM) if i in hbm else value
        for i, value in enumerate(args)
    ]

    def body(*refs):
        ins, results = list(refs[: len(args)]), refs[len(args) : len(args) + len(outs)]
        refs = refs[len(args) + len(outs) :]
        for place, i in enumerate(hbm):
            ins[i] = Arriving(ins[i], refs[place], refs[len(hbm)].at[place])
        kernel(*ins, *results, *refs[len(hbm) + 1 if hbm else 0 :])

    return pl.pallas_call(
        body,
        out_shape=[jax.ShapeDtypeStruct(shape, dtype) for shape, dtype in outs],
        in_specs=[
            pl.BlockSpec(memory_space=pltpu.HBM if i in hbm else pltpu.VMEM) for i in range(len(args))
        ],
        out_specs=[pl.BlockSpec(memory_space=pltpu.VMEM) for _ in outs],
        scratch_shapes=[pltpu.VMEM(args[i].shape, args[i].dtype) for i in hbm]
        + ([pltpu.SemaphoreType.DMA((len(hbm),))] if hbm else [])
        + [pltpu.VMEM(shape, dtype) for shape, dtype in scratch],
        compiler_params=pltpu.CompilerParams(vmem_limit_bytes=mib * 1024 * 1024),
        name=name,
    )(*args)


def tril(count):
    row = lax.broadcasted_iota(jnp.int32, (count, count), 0)
    col = lax.broadcasted_iota(jnp.int32, (count, count), 1)
    return row >= col


def cumulated(counts):
    length = counts.shape[1]
    row = lax.broadcasted_iota(jnp.int32, (length, length), 0)
    col = lax.broadcasted_iota(jnp.int32, (length, length), 1)
    ones = jnp.where(row <= col, 1.0, 0.0).astype(BF16)
    return dot(jnp.broadcast_to(counts, (8, length)), ones)


def embed(first_node, nodes, spans, sib, gain):
    feat, start = None, None
    for starts, ends, rows in spans:
        node = first_node + lax.broadcasted_iota(jnp.int32, (nodes, starts.shape[1]), 0)
        begun = starts <= node
        held = jnp.where(begun & (node < ends), 1.0, 0.0).astype(BF16)
        part = dot(held, rows)
        feat = part if feat is None else feat + part
        latest = jnp.max(jnp.where(begun, starts, -(2**30)), axis=1, keepdims=True)
        start = latest if start is None else jnp.maximum(start, latest)
    lanes = lax.broadcasted_iota(jnp.int32, (nodes, 128), 1)
    rank = first_node + lax.broadcasted_iota(jnp.int32, (nodes, 128), 0) - start
    onehot = jnp.where(rank == lanes, 1.0, 0.0).astype(BF16)
    feat = feat + dot(onehot[:, : sib.shape[0]], sib)
    inputs = feat.astype(BF16)
    x = inputs.astype(F32)
    inv = lax.rsqrt(jnp.mean(x * x, axis=-1, keepdims=True) + 1e-06)
    return inputs, x * inv * gain, onehot


def early_kernel(counts, rows, sib, gain, w_qkv, states_o, first_o, message_o, total):
    width = rows.shape[1]
    head = width // HEADS
    block = first_o.shape[0] // 2
    total[...] = jnp.zeros_like(total)
    first_o[...] = jnp.zeros_like(first_o)
    ends = cumulated(counts[...].astype(F32).astype(BF16))
    last = jnp.max(ends)
    number = last.astype(jnp.int32)
    ends = ends[0:1, :].astype(jnp.int32)
    starts = ends - counts[...]
    for value in (rows, sib, gain, w_qkv):
        value.ready()
    parents = rows.shape[0]
    message_o[:parents, :] = rows[...]
    message_o[parents:, :] = jnp.zeros((16, width), BF16)
    message_o[parents:, :parents] = jnp.broadcast_to(counts[...], (16, parents)).astype(F32).astype(BF16)

    def one(step, unused):
        _, normed, _ = embed(step * block, block, [(starts, ends, rows[...])], sib[...], gain[...])
        node = step * block + lax.broadcasted_iota(jnp.int32, (block, 1), 0)
        normed = jnp.where(node < number, normed, 0.0).astype(BF16)
        both = dot(normed, w_qkv[:, width:]).astype(BF16)
        for h in range(HEADS):
            cols = slice(h * head, (h + 1) * head)
            total[cols, :] += dot_tn(both[:, cols], both[:, width + h * head : width + (h + 1) * head])

        @pl.when(step < 2)
        def _():
            first_o[pl.ds(pl.multiple_of(step * block, block), block), :] = both

        return unused

    lax.fori_loop(0, (number + block - 1) // block, one, 0)
    states_o[:width, :] = total[...].astype(BF16)
    upper = jnp.floor(last * (1.0 / 256.0))
    row = lax.broadcasted_iota(jnp.int32, (16, 128), 0)
    states_o[width:, :] = jnp.where(row < 8, upper, last - 256.0 * upper).astype(BF16)


def assemble(core, half, far, other, later, whole):
    rows = far.shape[0]
    whole[pl.ds(pl.multiple_of(core * rows, rows), rows), :] = half[:rows, :]
    whole[pl.ds(pl.multiple_of((1 - core) * rows, rows), rows), :] = far[...].astype(F32)
    near = core == 0 if later else core == 1
    whole[...] += jnp.where(near, other[: 2 * rows, :].astype(F32), 0.0)


def main_kernel(
    scale, half, far, other, first, beside, mid, beyond, counts, occupancy, sib, gain, w_qkv, w_out, w_head,
    inputs_o, normed_o, rank_o, packed_o, prefix_o, attended_o, d_resid_o, grads_o, states_o, head_o, whole, readout,
):
    nodes, width = inputs_o.shape
    head = width // HEADS
    parents = mid.shape[0]
    place = lax.axis_index("seq")
    core = place % 2
    base = (place * nodes).astype(F32)
    assemble(core, half, far, other, False, whole)
    offset = half[width // 2 :, :] + jnp.where(core == 1, count_of(other[width:, :]), 0.0)
    shift = (offset - base)[0:1, 0:1]
    low = jnp.where(core == 0, beyond[...], beside[...])
    high = jnp.where(core == 0, beside[...], beyond[...])
    cum_low = cumulated(low[parents : parents + 1, :parents])[0:1, :]
    cum_mid = cumulated(counts[...].astype(F32).astype(BF16))[0:1, :]
    cum_high = cumulated(high[parents : parents + 1, :parents])[0:1, :]
    number_low = jnp.max(cum_low, axis=1, keepdims=True)
    number_mid = jnp.max(cum_mid, axis=1, keepdims=True)
    count_mid = counts[...].astype(F32)
    spans = []
    for cum, moved, each, rows in (
        (cum_low, -number_low, low[parents : parents + 1, :parents].astype(F32), low),
        (cum_mid, 0.0, count_mid, mid),
        (cum_high, number_mid, high[parents : parents + 1, :parents].astype(F32), high),
    ):
        ends = cum + (moved + shift)
        spans.append(((ends - each).astype(jnp.int32), ends.astype(jnp.int32), rows[:parents, :]))
    inputs, normed, onehot = embed(0, nodes, spans, sib[...], gain[...])
    normed = normed.astype(BF16)
    inputs_o[...] = inputs
    normed_o[...] = normed
    rank_o[...] = onehot
    packed = dot(normed, w_qkv[...]).astype(BF16)
    packed_o[...] = packed
    node = lax.broadcasted_iota(jnp.int32, (nodes, 1), 0)
    early = shift.astype(jnp.int32)
    causal = tril(nodes)
    nhats, invs = [], []
    for h in range(HEADS):
        cols = slice(h * head, (h + 1) * head)
        q = packed[:, cols]
        k = packed[:, width + h * head : width + (h + 1) * head]
        v = packed[:, 2 * width + h * head : 2 * width + (h + 1) * head]
        add = jnp.where(node < -early, first[:, cols], 0.0).astype(BF16)
        drop = jnp.where(node < early, k, 0.0).astype(BF16)
        state = whole[cols, :] + dot_tn(add, first[:, width + h * head : width + (h + 1) * head]) - dot_tn(drop, v)
        state = state.astype(BF16)
        prefix_o[cols, :] = state
        score = jnp.where(causal, dot_nt(q, k), 0.0).astype(BF16)
        numer = dot(score, v) + dot(q, state)
        inv = lax.rsqrt(jnp.mean(numer * numer, axis=-1, keepdims=True) + 1e-05)
        nhat = numer * inv
        nhats.append(nhat)
        invs.append(inv)
        attended_o[:, cols] = nhat.astype(BF16)
    resid = inputs.astype(F32) + dot(attended_o[...], w_out[...])
    inv_out = lax.rsqrt(jnp.mean(resid * resid, axis=-1, keepdims=True) + 1e-06)
    normal = resid * inv_out
    final = normal.astype(BF16)
    readout[...] = jnp.zeros_like(readout)
    readout[HEAD_AT : HEAD_AT + BITS, :] = w_head[...]
    logits = dot_nt(final, readout[...])
    lane = lax.broadcasted_iota(jnp.int32, logits.shape, 1) - HEAD_AT
    used = (lane >= 0) & (lane < BITS)
    bit = jnp.clip(lax.broadcasted_iota(jnp.int32, (128, nodes), 0) - HEAD_AT, 0, BITS - 1)
    target = (jnp.right_shift(occupancy[...], bit) & 1).astype(F32).T
    d_logits = jnp.where(used, (jax.nn.sigmoid(logits) - target) * scale, 0.0).astype(BF16)
    head_o[...] = dot_tn(final, d_logits)
    d_final = dot(d_logits, readout[...])
    d_resid = inv_out * (d_final - normal * jnp.mean(d_final * normal, axis=-1, keepdims=True))
    d_resid_o[...] = d_resid
    d_att = dot_nt(d_resid.astype(BF16), w_out[...])
    for h in range(HEADS):
        cols = slice(h * head, (h + 1) * head)
        e = d_att[:, cols]
        g = invs[h] * (e - nhats[h] * jnp.mean(e * nhats[h], axis=-1, keepdims=True))
        g = g.astype(BF16)
        grads_o[:, cols] = g
        states_o[cols, :] = dot_tn(packed[:, cols], g).astype(BF16)


def query_kernel(
    packed, grads, prefix, normed, attended, d_resid, w_qkv, d_normed_o, keep_o, send_o, whole
):
    nodes, width = grads.shape
    head = width // HEADS
    causal = tril(nodes)
    dqs = []
    for h in range(HEADS):
        cols = slice(h * head, (h + 1) * head)
        k = packed[:, width + h * head : width + (h + 1) * head]
        v = packed[:, 2 * width + h * head : 2 * width + (h + 1) * head]
        g = grads[:, cols]
        back = jnp.where(causal, dot_nt(g, v), 0.0).astype(BF16)
        dqs.append((dot(back, k) + dot_nt(g, prefix[cols, :])).astype(BF16))
    dq = jnp.concatenate(dqs, axis=1)
    d_normed_o[...] = dot_nt(dq, w_qkv[:, :width])
    whole[:, :width] = dot_tn(normed[...], dq)
    whole[:, width:] = dot_tn(attended[...], d_resid[...].astype(BF16))
    split(whole, keep_o, send_o)


def local_kernel(packed, grads, dk_o, dv_o):
    nodes, width = grads.shape
    head = width // HEADS
    causal = tril(nodes)
    for h in range(HEADS):
        cols = slice(h * head, (h + 1) * head)
        q = packed[:, cols]
        k = packed[:, width + h * head : width + (h + 1) * head]
        v = packed[:, 2 * width + h * head : 2 * width + (h + 1) * head]
        g = grads[:, cols]
        back = jnp.where(causal, dot_nt(g, v), 0.0).astype(BF16)
        dk_o[:, cols] = dot_tn(back, q)
        score = jnp.where(causal, dot_nt(q, k), 0.0).astype(BF16)
        dv_o[:, cols] = dot_tn(score, g)


def split(whole, keep_o, send_o):
    core = digit(1, 2)
    rows = keep_o.shape[0]
    keep_o[...] = whole[pl.ds(pl.multiple_of(core * rows, rows), rows), :]
    send_o[...] = whole[pl.ds(pl.multiple_of((1 - core) * rows, rows), rows), :]


def keys_kernel(packed, dk, dv, half, far, other, normed, both_o, keep_o, send_o, whole, suffix):
    nodes, width = dk.shape
    head = width // HEADS
    assemble(digit(1, 2), half, far, other, True, suffix)
    for h in range(HEADS):
        cols = slice(h * head, (h + 1) * head)
        k = packed[:, width + h * head : width + (h + 1) * head]
        v = packed[:, 2 * width + h * head : 2 * width + (h + 1) * head]
        state = suffix[cols, :].astype(BF16)
        both_o[:, cols] = (dk[:, cols] + dot_nt(v, state)).astype(BF16)
        both_o[:, width + h * head : width + (h + 1) * head] = (dv[:, cols] + dot(k, state)).astype(BF16)
    whole[...] = dot_tn(normed[...], both_o[...])
    split(whole, keep_o, send_o)


def halved(value):
    upper = value.astype(BF16)
    return upper, (value - upper.astype(F32)).astype(BF16)


def inputs_kernel(both, inputs, d_normed_q, d_resid, rank, gain, w_qkv, head, keep_o, send_o, whole):
    nodes, width = inputs.shape
    d_normed = d_normed_q[...] + dot_nt(both[...], w_qkv[:, width:])
    x = inputs[...].astype(F32)
    inv = lax.rsqrt(jnp.mean(x * x, axis=-1, keepdims=True) + 1e-06)
    unit = x * inv
    lanes = lax.broadcasted_iota(jnp.int32, (nodes, 128), 1)
    ninth = jnp.where(lanes == GAIN_AT, 1.0, 0.0).astype(BF16)
    s = d_normed * gain[...]
    d_inputs = inv * (s - unit * jnp.mean(s * unit, axis=-1, keepdims=True)) + d_resid[...]
    columns = head[...]
    for value, picked in ((d_inputs, jnp.where(lanes < GAIN_AT, rank[...], 0.0).astype(BF16)), (d_normed * unit, ninth)):
        for part in halved(value):
            columns = columns + dot_tn(part, picked)
    whole[...] = columns
    split(whole, keep_o, send_o)


def coded(value):
    lanes = lax.broadcasted_iota(jnp.int32, value.shape, 1)
    value = jnp.where(lanes < 64, value, 0.0)
    upper = value.astype(BF16).astype(F32)
    return (upper + pltpu.roll(value - upper, 64, 1)).astype(BF16)


def decoded(piece):
    piece = piece.astype(F32)
    return piece + pltpu.roll(piece, 64, 1)


def summed(main, at, held, heard, small):
    value = pair_sum([held[at, :main]] + [piece[at, :main].astype(F32) for piece in heard])
    if not small:
        return value, None
    return value, pair_sum([held[at, main:]] + [decoded(piece[at, main:]) for piece in heard])


def chunks_kernel(stride, radix, main, joined, *refs):
    ins, outs = refs[:-radix], refs[-radix:]
    rows, columns = outs[0].shape
    for b in range(radix):
        at = pl.ds(pl.multiple_of((digit(stride, radix) ^ b) * rows, rows), rows)
        if joined:
            value = ins[0][at, :] + ins[1][at, :]
            small = ins[2][at, :] + ins[3][at, :]
        else:
            value, small = summed(main, at, ins[0], ins[1:], columns > main)
        if b == 0:
            outs[0][:, :main] = value
            if small is not None:
                outs[0][:, main:] = small
        else:
            outs[b][:, :main] = value.astype(BF16)
            if small is not None:
                outs[b][:, main:] = coded(small)


def piece_kernel(main, *refs):
    out = refs[-1]
    rows, columns = out.shape
    value, small = summed(main, slice(0, rows), refs[0], refs[1:-1], columns > main)
    out[:, :main] = value.astype(BF16)
    if small is not None:
        out[:, main:] = coded(small)


def scatter_step(ins, rows, columns, main, joined, stride, radix):
    outs = [((rows, columns), F32)] + [((rows, columns), BF16)] * (radix - 1)
    got = call(
        functools.partial(chunks_kernel, stride, radix, main, joined), outs, *ins, name="chunks", mib=8
    )
    return got[0], swap_each(got[1:], stride, radix)


def reduce_scatter(keep, send, small=None):
    stages = stages_of(lax.axis_size("seq"))
    rows, main = keep.shape
    ins = [keep] + swap(send, *stages[0])
    columns = main
    if small is not None:
        ins = ins + [small[0]] + swap(small[1], *stages[0])
        columns = main + 128
    used = []
    for stride, radix in stages[1:]:
        joined = not used and small is not None
        if rows % (16 * radix) == 0:
            rows = rows // radix
            held, heard = scatter_step(ins, rows, columns, main, joined, stride, radix)
            used.append((stride, radix))
        else:
            parts = [ins[0][:, :main]] + [piece[:, :main].astype(F32) for piece in ins[1:]]
            held = pair_sum(parts)
            if columns > main:
                parts = [piece[:, main:].astype(F32) for piece in ins[1:]]
                parts = pair_sum([ins[0][:, main:]] + [part + jnp.roll(part, 64, 1) for part in parts])
                held = jnp.concatenate([held, jnp.where(jnp.arange(128) < 64, parts, 0.0)], axis=1)
            heard = swap(held, stride, radix)
        ins = [held] + heard
    (piece,) = call(functools.partial(piece_kernel, main), [((rows, columns), BF16)], *ins, name="piece", mib=4)
    return piece, used


def join_kernel(*refs):
    rows = refs[0].shape[0]
    for i, piece in enumerate(refs[:-1]):
        refs[-1][i * rows : (i + 1) * rows, :] = piece[...]


def gather(piece, used):
    for stride, radix in reversed(used):
        pieces = [piece] + swap(piece, stride, radix)
        shape = (radix * piece.shape[0], piece.shape[1])
        (piece,) = call(join_kernel, [(shape, BF16)], *pieces, name="join", mib=4)
    return piece, swap(piece, *stages_of(lax.axis_size("seq"))[0])[0]


def place_kernel(stages, first, first_far, second, second_far, qkv_o, out_o, head_o, gain_o, sib_o, small):
    width = out_o.shape[1]
    half = first.shape[0]
    core = digit(1, 2)
    blocks = 1
    for _, radix in stages:
        blocks *= radix
    rows = half // blocks
    for index in range(blocks):
        left, target, size, inner = index, 0, half, blocks
        for stride, radix in stages:
            inner //= radix
            b = left // inner
            left = left % inner
            size = size // radix
            target = target + (digit(stride, radix) ^ b) * size
        src = slice(index * rows, (index + 1) * rows)
        near = pl.ds(pl.multiple_of(core * half + target, rows), rows)
        far = pl.ds(pl.multiple_of((1 - core) * half + target, rows), rows)
        for at, one, two in ((near, first, second), (far, first_far, second_far)):
            qkv_o[at, :width] = one[src, :width].astype(F32)
            out_o[at, :] = one[src, width:].astype(F32)
            qkv_o[at, width:] = two[src, : 2 * width].astype(F32)
            small[at, :] = decoded(two[src, 2 * width :])
    columns = small[...]
    across = columns.T
    head_o[...] = across[HEAD_AT : HEAD_AT + BITS, :]
    sib_o[...] = across[: sib_o.shape[0], :]
    gain_o[...] = across[GAIN_AT : GAIN_AT + 1, :]


def shards(parent_rows, counts, occupancy, sib_table, gain, w_qkv, w_out, w_head):
    count = lax.axis_size("seq")
    parents = counts.shape[0]
    nodes = occupancy.shape[0]
    width = parent_rows.shape[1]
    head = width // HEADS
    across = [(i, i + 1 if i % 2 else i - 1) for i in range(1, count - 1)]
    count_row = counts.reshape(1, parents)
    gain_row = gain.reshape(1, width)

    states, first, message = call(
        early_kernel,
        [((width + 16, head), BF16), ((nodes, 2 * width), BF16), ((parents + 16, width), BF16)],
        count_row, parent_rows, sib_table, gain_row, w_qkv,
        hbm=range(5),
        scratch=[((width, head), F32)],
        name="early",
    )
    beside = swap(message, 1, 2)[0]
    beyond = lax.ppermute(message, "seq", across)
    half, far, other = scan_states(states, False, True)

    scale = float(count * nodes) ** (-0.5)
    inputs, normed, rank, packed, prefix, attended, d_resid, grads, qstates, grad_head = call(
        functools.partial(main_kernel, scale),
        [
            ((nodes, width), BF16),
            ((nodes, width), BF16),
            ((nodes, 128), BF16),
            ((nodes, 3 * width), BF16),
            ((width, head), BF16),
            ((nodes, width), BF16),
            ((nodes, width), F32),
            ((nodes, width), BF16),
            ((width, head), BF16),
            ((width, 128), F32),
        ],
        half, far, other, first, beside, parent_rows, beyond, count_row,
        occupancy.reshape(1, nodes), sib_table, gain_row, w_qkv, w_out, w_head.T,
        scratch=[((width, head), F32), ((128, width), BF16)],
        name="main",
        mib=32,
    )
    half, far, other = scan_states(qstates, True, False)

    halves = [((width // 2, 2 * width), F32)] * 2
    d_normed_q, keep, send = call(
        query_kernel,
        [((nodes, width), F32)] + halves,
        packed, grads, prefix, normed, attended, d_resid, w_qkv,
        scratch=[((width, 2 * width), F32)],
        name="query",
        mib=16,
    )
    dk, dv = call(local_kernel, [((nodes, width), F32)] * 2, packed, grads, name="local")
    piece, used = reduce_scatter(keep, send)
    gathered, gathered_far = gather(piece, used)

    both, keep, send = call(
        keys_kernel,
        [((nodes, 2 * width), BF16)] + halves,
        packed, dk, dv, half, far, other, normed,
        scratch=[((width, 2 * width), F32), ((width, head), F32)],
        name="keys",
        mib=16,
    )
    small = call(
        inputs_kernel,
        [((width // 2, 128), F32)] * 2,
        both, inputs, d_normed_q, d_resid, rank, gain_row, w_qkv, grad_head,
        scratch=[((width, 128), F32)],
        name="inputs",
    )
    piece, used = reduce_scatter(keep, send, small)
    second, second_far = gather(piece, used)

    grad_qkv, grad_out, grad_head, grad_gain, grad_sib = call(
        functools.partial(place_kernel, used),
        [
            ((width, 3 * width), F32),
            ((width, width), F32),
            ((BITS, width), F32),
            ((1, width), F32),
            ((sib_table.shape[0], width), F32),
        ],
        gathered, gathered_far, second, second_far,
        scratch=[((width, 128), F32)],
        name="place",
        mib=16,
    )
    return grad_qkv, grad_out, grad_head.T, grad_gain.reshape(width), grad_sib


def solution(mesh):
    placed = (P("seq", None), P("seq"), P("seq"), P(), P(), P(), P(), P())
    return jax.shard_map(
        shards, mesh=mesh, in_specs=placed, out_specs=(P(), P(), P(), P(), P()), check_vma=False
    )
```
